512 devices in a mesh: band: 4 (over y_hi), row: 32 (over z, x), col: 4 (over y_lo, core).
Axes of the slice: x: 4, y: 8 (y_hi: 4, y_lo: 2; y = y_hi * 2 + y_lo), z: 8, core: 2. Of those that a mesh axis runs over, the one named last changes fastest.
Arguments:
- spectral_cube: bfloat16 [88, 128, 4096], P('band', ('row', 'col')), may hold values from -6 to 6
- aperture: int32 [128, 4096], P(('row', 'col')), may hold values 0 or 1
- measurement: float32 [128, 4444], P(('row', 'col')), may hold values from -48 to 48
- shears: int32 [88], P('band'), may hold values from 0 to 348, as said below
- step_sizes: float32 [88], P('band'), may hold values from 0.5 to 2
- spatial_weight: bfloat16 [16, 9], replicated, may hold values from -2 to 2
- spatial_bias: float32 [16], replicated, may hold values from -3 to 3
- spectral_weight: bfloat16 [7, 16, 16], replicated, may hold values from -0.5 to 0.5
- spectral_bias: float32 [16], replicated, may hold values from -3 to 3
- out_weight: float32 [16], replicated, may hold values from -1.5 to 1.5
Outputs:
- denoised: bfloat16 [88, 128, 4096], P('band', ('row', 'col'))
The draws below stay inside these ranges and needn't reach their ends.
Inputs may be any that keep to these rules, and one draw needn't show every extreme that they name: `shears`: strictly increasing over the bands, the first 0 and the last 348.
All inputs are finite; a program needn't handle non-finite values. No bound on the sum of `aperture` on one device may be relied on, other than what follows from the above.
Results may differ from the reference program's by a relative error of at most 0.0047.
Values may be sent and summed in bfloat16 or wider, within the bound.
A program may use at most 64 MiB of HBM per device.

```python
import math
import jax
import jax.numpy as jnp
from jax import lax

COLS = 4096
CH = 16
TAPS = 7
BANDS = 88
SHEAR = 348
ROWS = 128


def draw_shears(key, part):
    gaps = BANDS - 1
    base_step = SHEAR // gaps
    extra = SHEAR - base_step * gaps
    quarter = gaps // 4
    ranks = jax.random.permutation(key, gaps)
    change = jnp.where(ranks < quarter, 1, jnp.where(ranks < 2 * quarter, -1, 0))
    last_extra = jnp.where(jnp.arange(gaps) == gaps - 1, extra, 0)
    increments = (base_step + change + last_extra).astype(jnp.int32)
    return jnp.concatenate([jnp.zeros((1,), jnp.int32), jnp.cumsum(increments).astype(jnp.int32)])


def with_ends(result, stream_key, low, high):
    shape = result.shape
    spot = [jax.random.randint(jax.random.fold_in(stream_key, axis), (), 0, shape[axis]) for axis in range(len(shape))]
    result = result.at[tuple(spot)].set(low)
    longest = shape.index(max(shape))
    spot[longest] = (spot[longest] + 1) % shape[longest]
    return result.at[tuple(spot)].set(high)


def steps_of(stream_key, shape, cuts, least, largest):
    def one(position, blocks):
        steps = jax.random.uniform(jax.random.fold_in(jax.random.fold_in(stream_key, 6), position), (blocks,), jnp.float32, least / len(cuts), largest / len(cuts))
        return jnp.repeat(jnp.exp(steps), shape[position] // blocks).reshape((-1,) + (1,) * (len(shape) - position - 1))

    factor_of = one(*cuts[0])
    for cut in cuts[1:]:
        factor_of = factor_of * one(*cut)
    return factor_of


def normal_values(key, dims, spread, reach, cuts=(), kind=jnp.bfloat16):
    entries = spread * jax.random.normal(key, dims, jnp.float32)
    if cuts:
        entries = entries * steps_of(key, dims, cuts, -0.22, 0.18)
    return jnp.clip(entries, -reach, reach).astype(kind)


def setup_inputs(seed: int = 0) -> dict:
    seeds = jax.random.split(jax.random.key(seed), 11)
    return {
        "spectral_cube": normal_values(seeds[0], (BANDS, ROWS, COLS), 1.0, 6.0, ((0, 4), (1, 128))),
        "aperture": with_ends((jax.random.randint(seeds[1], (ROWS, COLS), 0, 2) < 1).astype(jnp.int32), jax.random.fold_in(seeds[1], 1), 0, 1),
        "measurement": normal_values(seeds[2], (ROWS, COLS + SHEAR), 8.0, 48.0, ((0, 128),), jnp.float32),
        "shears": draw_shears(jax.random.fold_in(seeds[10], 71), 0),
        "step_sizes": jnp.clip(jnp.exp(math.log(2.0) - 1.3862944 * jax.random.uniform(seeds[4], (BANDS,), jnp.float32) ** steps_of(seeds[4], (BANDS,), ((0, 4),), -0.2, 0.2)), 0.5, 2.0),
        "spatial_weight": normal_values(seeds[5], (CH, 9), 9 ** -0.5, 2.0),
        "spatial_bias": normal_values(seeds[6], (CH,), 0.5, 3.0, (), jnp.float32),
        "spectral_weight": normal_values(seeds[7], (TAPS, CH, CH), (TAPS * CH) ** -0.5, 0.5),
        "spectral_bias": normal_values(seeds[8], (CH,), 0.5, 3.0, (), jnp.float32),
        "out_weight": normal_values(seeds[9], (CH,), CH ** -0.5, 1.5, (), jnp.float32),
    }


def denoise(padded, band_start, total_bands, block_width, spatial_weight, spatial_bias, spectral_weight, spectral_bias, out_weight):
    bands_in, rows_pad, cols_pad = padded.shape
    row_count = rows_pad - 2
    col_count = cols_pad - 2
    bands_out = bands_in - 6
    across = col_count // block_width
    band_ids = band_start + jnp.arange(bands_in, dtype=jnp.int32)
    band_valid = (band_ids >= 0) & (band_ids < total_bands)
    weight_f = out_weight.astype(jnp.float32)

    def one_block(block_index):
        row_index = block_index // across
        col_start = (block_index % across) * block_width
        window = lax.dynamic_slice(padded, (jnp.int32(0), row_index, col_start), (bands_in, 3, block_width + 2))
        patches = jnp.stack([window[:, i, j:j + block_width] for i in range(3) for j in range(3)])
        spatial_out = jnp.einsum("kq,qbc->kbc", spatial_weight, patches, preferred_element_type=jnp.float32) + spatial_bias[:, None, None]
        active = jnp.where(band_valid[None, :, None], jax.nn.silu(spatial_out), 0.0).astype(jnp.bfloat16)
        second = jnp.zeros((spatial_out.shape[0], bands_out, block_width), jnp.float32) + spectral_bias[:, None, None]
        for d in range(spectral_weight.shape[0]):
            second = second + jnp.einsum("kj,jbc->kbc", spectral_weight[d], active[:, d:d + bands_out], preferred_element_type=jnp.float32)
        update_term = jnp.einsum("k,kbc->bc", weight_f, jax.nn.silu(second), precision=lax.Precision.HIGHEST)
        center = window[3:3 + bands_out, 1, 1:1 + block_width].astype(jnp.float32)
        return (center + update_term).astype(jnp.bfloat16)

    blocks = lax.map(one_block, jnp.arange(row_count * across, dtype=jnp.int32))
    return blocks.reshape(row_count, across, bands_out, block_width).transpose(2, 0, 1, 3).reshape(bands_out, row_count, col_count)


def reference(spectral_cube, aperture, measurement, shears, step_sizes, spatial_weight, spatial_bias, spectral_weight, spectral_bias, out_weight):
    detector_width = COLS + SHEAR
    aperture_f = aperture.astype(jnp.float32)
    masked = spectral_cube.astype(jnp.float32) * aperture_f[None]

    def place(carry, inputs):
        band_layer, offset = inputs
        empty_plane = jnp.zeros((ROWS, detector_width), jnp.float32)
        placed_band = lax.dynamic_update_slice(empty_plane, band_layer, (jnp.int32(0), offset))
        opened = lax.dynamic_update_slice(empty_plane, aperture_f, (jnp.int32(0), offset))
        return (carry[0] + placed_band, carry[1] + opened), None

    start_sums = (jnp.zeros((ROWS, detector_width), jnp.float32), jnp.zeros((ROWS, detector_width), jnp.float32))
    (predicted, counts), _ = lax.scan(place, start_sums, (masked, shears))
    residual = (measurement - predicted) / jnp.maximum(counts, 1.0)

    def adjoint(inputs):
        offset, step_one = inputs
        pulled = lax.dynamic_slice(residual, (jnp.int32(0), offset), (ROWS, COLS))
        return pulled * aperture_f * step_one

    updates = lax.map(adjoint, (shears, step_sizes))
    updated = (spectral_cube.astype(jnp.float32) + updates).astype(jnp.bfloat16)
    padded = jnp.pad(updated, ((3, 3), (1, 1), (1, 1)))
    return denoise(padded, -3, BANDS, COLS, spatial_weight, spatial_bias, spectral_weight, spectral_bias, out_weight)
```

```python
import jax
import jax.numpy as jnp
from jax import lax
from jax.experimental import pallas as pl
from jax.experimental.pallas import tpu as pltpu
from jax.sharding import PartitionSpec as P

MESH = pl.DeviceIdType.MESH
F32 = jnp.float32
BF16 = jnp.bfloat16
LANES = 128
BANDS = 22
HALO = 3
CH = 16
SLOTS = 28
ACT = SLOTS * CH
TILE = 256


def iota(shape, dim):
    return lax.broadcasted_iota(jnp.int32, shape, dim)


def column_of(row, rows, where):
    shape = (rows, row.shape[1])
    return jnp.sum(
        jnp.where(where(iota(shape, 0), iota(shape, 1)), row, 0.0), axis=1, keepdims=True
    )


def pieces(x):
    high = x.astype(BF16).astype(F32)
    middle = (x - high).astype(BF16).astype(F32)
    return high, middle, x - high - middle


def gather_lanes(x, index):
    return jnp.take_along_axis(x, index, axis=1, mode="promise_in_bounds")


def project(cube, aperture, shears, part):
    rows = 24
    tiles = cube.shape[1] // LANES
    shift = column_of(shears[...].astype(F32), rows, lambda i, l: i == l).astype(jnp.int32)
    lane = iota((rows, LANES), 1)
    within = jnp.broadcast_to(shift & (LANES - 1), (rows, LANES))
    index = (lane - within) & (LANES - 1)
    steps = (shift >> 7) + jnp.where(lane < within, 1, 0)
    own = iota((rows, LANES), 0) < BANDS
    masked, opened = [], []
    none = jnp.zeros((rows, LANES), F32)
    for t in range(part.shape[1] // LANES):
        if t < tiles:
            at = slice(t * LANES, (t + 1) * LANES)
            open_t = aperture[:, at].astype(F32)
            band_t = jnp.concatenate([cube[:, at].astype(F32), jnp.zeros((rows - BANDS, LANES), F32)])
            masked.append(gather_lanes(band_t * open_t, index))
            opened.append(gather_lanes(jnp.where(own, open_t, 0.0), index))
        else:
            masked.append(none)
            opened.append(none)
        for row, placed in enumerate((masked, opened)):
            back = [placed[t - e] if t >= e else none for e in range(4)]
            here = jnp.where(
                steps == 0, back[0], jnp.where(steps == 1, back[1], jnp.where(steps == 2, back[2], back[3]))
            )
            part[row : row + 1, t * LANES : (t + 1) * LANES] = jnp.sum(
                here, axis=0, keepdims=True
            ).astype(part.dtype)


def pack_small(shears, steps, small):
    small[...] = jnp.zeros_like(small)
    small[0:1, 0:BANDS] = shears[...].astype(F32)
    small[1:2, 0:BANDS] = steps[...]


def pack_edges(cube, low, high):
    for t in range(0, cube.shape[1], 512):
        at = slice(t, t + 512)
        bands = cube[:, at].astype(F32)
        none = jnp.zeros((1, 512), F32)
        low[:, at] = jnp.concatenate([bands[0:HALO], none]).astype(BF16)
        high[:, at] = jnp.concatenate([bands[BANDS - HALO :], none]).astype(BF16)


def expand_spatial(weight, bias, band, groups, one, two):
    half = 0.5 * column_of(bias[...], CH, lambda i, l: i == l)
    parts = pieces(half)
    taps = weight.shape[1]
    depth = (taps + 1) * CH
    spread = (iota((taps, depth), 1) // CH == iota((taps, depth), 0)).astype(BF16)
    wide = jnp.dot(weight[...] * jnp.bfloat16(0.5), spread, preferred_element_type=F32)
    col = iota((CH, depth), 1)
    bias_row = jnp.where(
        col == taps * CH,
        parts[0],
        jnp.where(col == taps * CH + 1, parts[1], jnp.where(col == taps * CH + 2, parts[2], 0.0)),
    )
    in_taps = col < taps * CH
    slot = col & (CH - 1)

    def block(wanted):
        return jnp.where(in_taps, jnp.where(slot == wanted, wide, 0.0), bias_row)

    for b in range(CH):
        one[b * CH : (b + 1) * CH, :] = block(b).astype(BF16)
    slots = [0, 1, 2, 3, 4, 5, 8, 9, 10, 12, 13, 14]
    for n, s in enumerate(slots):
        value = block(s)
        if 8 <= s < 12:
            value = jnp.where(band > 0, value, 0.0)
        if s >= 12:
            value = jnp.where(band < groups - 1, value, 0.0)
        two[n * CH : (n + 1) * CH, :] = value.astype(BF16)


def expand_spectral(weight, bias, out):
    depth = out.shape[1]
    rows = 24
    half = 0.5 * column_of(bias[...], CH, lambda i, l: i == l)
    parts = pieces(half)
    spread = ((iota((CH, depth), 1) & (CH - 1)) == iota((CH, depth), 0)).astype(BF16)
    wide = jnp.dot(weight[...] * jnp.bfloat16(0.5), spread, preferred_element_type=F32)
    col = iota((rows, depth), 1)
    slot = col >> 4
    place = jnp.where(slot < BANDS, slot + HALO, jnp.where(slot < BANDS + HALO, slot - BANDS, slot))
    band = iota((rows, depth), 0)
    tap = jnp.where((slot < SLOTS) & (band < BANDS), place - band, -1)
    taps = weight.shape[0] // CH
    for k in range(CH):
        block = jnp.where(col == ACT, parts[0][k : k + 1], 0.0)
        block = jnp.where(col == ACT + 1, parts[1][k : k + 1], block)
        block = jnp.where(col == ACT + 2, parts[2][k : k + 1], block)
        for d in range(taps):
            block = jnp.where(tap == d, wide[d * CH + k : d * CH + k + 1], block)
        out[k * rows : (k + 1) * rows, :] = block.astype(BF16)


def refresh(cubes, apertures, lows, highs, residuals, smalls, row, rows, upd):
    width = cubes[0].shape[1]
    own, below, above = (s[...] for s in smalls)

    def column(n):
        return (
            column_of(own[n : n + 1], 32, lambda i, l: (i == l) & (i < BANDS))
            + column_of(below[n : n + 1], 32, lambda i, l: (i - 24 + BANDS - HALO == l) & (i >= 24) & (i < 24 + HALO))
            + column_of(above[n : n + 1], 32, lambda i, l: (i - 28 == l) & (i >= 28) & (i < 28 + HALO))
        )

    shift = column(0).astype(jnp.int32)
    step = jnp.broadcast_to(column(1), (32, LANES))
    lane = iota((32, LANES), 1)
    within = jnp.broadcast_to(shift & (LANES - 1), (32, LANES))
    index = (lane + within) & (LANES - 1)
    steps = (shift >> 7) + jnp.where(lane + within >= LANES, 1, 0)
    is0, is1, is2 = steps == 0, steps == 1, steps == 2
    margin = jnp.zeros((32, LANES), BF16)
    for i in range(3):
        upd[i, :, 0:LANES] = margin
        upd[i, :, LANES + width : 2 * LANES + width] = margin
        inside = (row + i >= 1) & (row + i <= rows)

        def pull(t, i=i):
            at = pl.ds(pl.multiple_of(t * LANES, LANES), LANES)
            return gather_lanes(jnp.broadcast_to(residuals[i][:, at], (32, LANES)), index)

        def tile(t, carry, i=i, inside=inside):
            p0, p1, p2 = carry
            p3 = pull(t + 3)
            at = pl.ds(pl.multiple_of(t * LANES, LANES), LANES)
            pulled = jnp.where(is0, p0, jnp.where(is1, p1, jnp.where(is2, p2, p3)))
            cube = jnp.concatenate(
                [
                    cubes[i][:, at].astype(F32),
                    jnp.zeros((2, LANES), F32),
                    lows[i][:, at].astype(F32),
                    highs[i][:, at].astype(F32),
                ]
            )
            new = cube + pulled * apertures[i][:, at].astype(F32) * step
            new = jnp.where(inside, new, 0.0)
            upd[i, :, pl.ds(pl.multiple_of(t * LANES + LANES, LANES), LANES)] = new.astype(BF16)
            return p1, p2, p3

        lax.fori_loop(0, width // LANES, tile, (pull(0), pull(1), pull(2)))


def denoise(upd, one, two, spectral, out_weight, active, out):
    width = out.shape[1]
    ones = jnp.ones((CH, TILE), BF16)
    active[ACT:, :] = ones
    project_out = column_of(out_weight[...], CH, lambda i, l: i == l)

    def tile(t, carry):
        start = pl.multiple_of(t * TILE, TILE)
        window = [upd[i, :, pl.ds(start, TILE + 2 * LANES)] for i in range(3)]
        shifted = [window[i][:, LANES - 1 + j : LANES - 1 + j + TILE] for i in range(3) for j in range(3)]
        for weight, group, at in ((one, slice(0, 16), 0), (two, slice(16, 32), 16 * CH)):
            patch = jnp.concatenate([s[group] for s in shifted] + [ones])
            half = jnp.dot(weight[...], patch, preferred_element_type=F32)
            active[at : at + half.shape[0], :] = (half * jnp.tanh(half) + half).astype(BF16)
        half = jnp.dot(spectral[...], active[...], preferred_element_type=F32)
        total = shifted[4].astype(F32)[0:24]
        for k in range(CH):
            h = half[k * 24 : (k + 1) * 24]
            total = total + project_out[k : k + 1] * (h * jnp.tanh(h) + h)
        out[:, pl.ds(start, TILE)] = total[0:BANDS].astype(BF16)
        return carry

    lax.fori_loop(0, width // TILE, tile, 0)


def prepare_kernel(groups, cube, aperture, shears, steps, sw, sb, pw, pb, part, low, high, small, one, two, spectral):
    project(cube, aperture, shears, part)
    pack_small(shears, steps, small)
    pack_edges(cube, low, high)
    expand_spatial(sw, sb, lax.axis_index("band"), groups, one, two)
    expand_spectral(pw, pb, spectral)


def exchange_kernel(
    sizes,
    cube, aperture, meas, part, low, high, small,
    cube_up, cube_down, ap_up, ap_down, lows, highs, small_low, small_high, res, res_up, res_down,
    parts, send, recv, barrier_dummy=None,
):
    groups, nrow, ncol = sizes
    band, row, col = lax.axis_index("band"), lax.axis_index("row"), lax.axis_index("col")
    count = nrow * ncol
    flat = row * ncol + col

    def device(db, dr):
        r = lax.rem(flat + dr + count, count)
        return (lax.rem(band + db + groups, groups), r // ncol, lax.rem(r, ncol))

    peers = [(db, dr) for db in (-1, 1) for dr in (-1, 0, 1)] + [(2, 0), (0, -1), (0, 1)]
    barrier = pltpu.get_barrier_semaphore()
    for peer in peers:
        pl.semaphore_signal(barrier, inc=1, device_id=device(*peer), device_id_type=MESH)
    pl.semaphore_wait(barrier, len(peers))

    used = [0]

    def copy(src, dst, peer):
        n = used[0]
        used[0] += 1
        return pltpu.make_async_remote_copy(
            src_ref=src, dst_ref=dst, send_sem=send.at[n], recv_sem=recv.at[n],
            device_id=device(*peer), device_id_type=MESH,
        )

    partial = [copy(part, parts.at[n], (db, 0)) for n, db in enumerate((1, 2, -1))]
    bulk = [
        copy(small, small_low, (1, 0)),
        copy(small, small_high, (-1, 0)),
        copy(aperture, ap_up, (0, 1)),
        copy(aperture, ap_down, (0, -1)),
    ]
    for dr in (0, 1, -1):
        bulk.append(copy(high, lows.at[1 - dr], (1, dr)))
        bulk.append(copy(low, highs.at[1 - dr], (-1, dr)))
    bulk += [copy(cube, cube_up, (0, 1)), copy(cube, cube_down, (0, -1))]
    last = [copy(res, res_up, (0, 1)), copy(res, res_down, (0, -1))]
    for c in partial + bulk:
        c.start()
    for c in partial:
        c.wait_recv()
    width = meas.shape[1]
    total = part[...].astype(F32) + (parts[0].astype(F32) + parts[1].astype(F32) + parts[2].astype(F32))
    predicted, counts = total[0:1, 0:width], total[1:2, 0:width]
    res[:, 4352:] = jnp.zeros((1, res.shape[1] - 4352), F32)
    res[:, 0:width] = (meas[...] - predicted) / jnp.maximum(counts, 1.0)
    for c in last:
        c.start()
    for c in bulk + last:
        c.wait_recv()
    for c in partial + bulk + last:
        c.wait_send()


def finish_kernel(sizes, *refs):
    (cube, cube_up, cube_down, ap, ap_up, ap_down, lows, highs, small, small_low, small_high,
     res, res_up, res_down, one, two, spectral, out_weight, out, upd, active) = refs
    groups, nrow, ncol = sizes
    flat = lax.axis_index("row") * ncol + lax.axis_index("col")
    refresh(
        (cube_up, cube, cube_down),
        (ap_up, ap, ap_down),
        [lows.at[i] for i in range(3)],
        [highs.at[i] for i in range(3)],
        (res_up, res, res_down),
        (small, small_low, small_high),
        flat,
        nrow * ncol,
        upd,
    )
    denoise(upd, one, two, spectral, out_weight, active, out)


def solution(mesh):
    sizes = tuple(mesh.shape[a] for a in ("band", "row", "col"))
    vmem = pl.BlockSpec(memory_space=pltpu.VMEM)

    def on_device(cube, aperture, meas, shears, steps, sw, sb, pw, pb, ow):
        width = cube.shape[2]
        cube = cube.reshape(cube.shape[0], width)
        shears, steps, sb, pb, ow = (a.reshape(1, -1) for a in (shears, steps, sb, pb, ow))
        pw = pw.reshape(-1, CH)
        wide = (meas.shape[1] + 2 * LANES - 1) // LANES * LANES
        shape = jax.ShapeDtypeStruct
        edge = shape((4, width), BF16)
        part, low, high, small, one, two, spectral = pl.pallas_call(
            lambda *r: prepare_kernel(sizes[0], *r),
            name="prepare",
            out_shape=(
                shape((2, wide), F32), edge, edge, shape((8, LANES), F32),
                shape((16 * CH, 10 * CH), BF16), shape((12 * CH, 10 * CH), BF16), shape((24 * CH, ACT + CH), BF16),
            ),
            in_specs=[vmem] * 8,
            out_specs=(vmem,) * 7,
        )(cube, aperture, shears, steps, sw, sb, pw, pb)
        row = shape((1, wide), F32)
        halos = pl.pallas_call(
            lambda *r: exchange_kernel(sizes, *r),
            name="exchange",
            out_shape=(
                shape(cube.shape, BF16), shape(cube.shape, BF16), shape(aperture.shape, jnp.int32), shape(aperture.shape, jnp.int32),
                shape((3, 4, width), BF16), shape((3, 4, width), BF16), shape((8, LANES), F32), shape((8, LANES), F32), row, row, row,
            ),
            in_specs=[vmem] * 7,
            out_specs=(vmem,) * 11,
            scratch_shapes=[
                pltpu.VMEM((3, 2, wide), F32),
                pltpu.SemaphoreType.DMA((17,)),
                pltpu.SemaphoreType.DMA((17,)),
            ],
            compiler_params=pltpu.CompilerParams(collective_id=0, has_side_effects=True),
        )(cube, aperture, meas, part, low, high, small)
        cube_up, cube_down, ap_up, ap_down, lows, highs, small_low, small_high, res, res_up, res_down = halos
        out = pl.pallas_call(
            lambda *r: finish_kernel(sizes, *r),
            name="finish",
            out_shape=shape(cube.shape, BF16),
            in_specs=[vmem] * 18,
            out_specs=vmem,
            scratch_shapes=[
                pltpu.VMEM((3, 32, width + 2 * LANES), BF16),
                pltpu.VMEM((ACT + CH, TILE), BF16),
            ],
        )(cube, cube_up, cube_down, aperture, ap_up, ap_down, lows, highs, small, small_low, small_high,
          res, res_up, res_down, one, two, spectral, ow)
        return out.reshape(out.shape[0], 1, width)

    in_specs = (
        P("band", ("row", "col"), None),
        P(("row", "col"), None),
        P(("row", "col"), None),
        P("band"),
        P("band"),
        P(),
        P(),
        P(),
        P(),
        P(),
    )
    return jax.shard_map(
        on_device, mesh=mesh, in_specs=in_specs, out_specs=P("band", ("row", "col"), None), check_vma=False
    )
```

```python
import jax
import jax.numpy as jnp
from jax import lax
from jax.experimental import pallas as pl
from jax.experimental.pallas import tpu as pltpu
from jax.sharding import PartitionSpec as P

MESH = pl.DeviceIdType.MESH
F32 = jnp.float32
BF16 = jnp.bfloat16
LANES = 128
BANDS = 22
HALO = 3
CH = 16
SLOTS = 28
ACT = SLOTS * CH
TILE = 256


def iota(shape, dim):
    return lax.broadcasted_iota(jnp.int32, shape, dim)


def column_of(row, rows, where):
    shape = (rows, row.shape[1])
    return jnp.sum(
        jnp.where(where(iota(shape, 0), iota(shape, 1)), row, 0.0), axis=1, keepdims=True
    )


def pieces(x):
    high = x.astype(BF16).astype(F32)
    middle = (x - high).astype(BF16).astype(F32)
    return high, middle, x - high - middle


def gather_lanes(x, index):
    return jnp.take_along_axis(x, index, axis=1, mode="promise_in_bounds")


def place(tiles, shift, out, tile_of):
    rows = shift.shape[0]
    lane = iota((rows, LANES), 1)
    within = jnp.broadcast_to(shift & (LANES - 1), (rows, LANES))
    index = (lane - within) & (LANES - 1)
    steps = (shift >> 7) + jnp.where(lane < within, 1, 0)
    is0, is1, is2 = steps == 0, steps == 1, steps == 2
    none = jnp.zeros((rows, LANES), F32)
    turned = []
    for t in range(out.shape[1] // LANES):
        turned.append(gather_lanes(tile_of(t), index) if t < tiles else none)
        back = [turned[t - e] if t >= e else none for e in range(4)]
        here = jnp.where(is0, back[0], jnp.where(is1, back[1], jnp.where(is2, back[2], back[3])))
        out[:, t * LANES : (t + 1) * LANES] = jnp.sum(here, axis=0, keepdims=True)


def shift_column(row):
    return column_of(row, 24, lambda i, l: i == l).astype(jnp.int32)


def project(cube, aperture, shears, part):
    def masked(t):
        at = slice(t * LANES, (t + 1) * LANES)
        bands = jnp.concatenate([cube[:, at].astype(F32), jnp.zeros((24 - BANDS, LANES), F32)])
        return bands * aperture[:, at].astype(F32)

    place(cube.shape[1] // LANES, shift_column(shears[...].astype(F32)), part, masked)


def count_open(aperture, smalls, out):
    shift = jnp.concatenate([shift_column(s[0:1]) for s in smalls])
    shape = (shift.shape[0], LANES)
    group_row = jnp.concatenate([iota((24, LANES), 0)] * len(smalls))
    own = group_row < BANDS

    def opened(t):
        open_t = aperture[:, t * LANES : (t + 1) * LANES].astype(F32)
        return jnp.where(own, jnp.broadcast_to(open_t, shape), 0.0)

    place(aperture.shape[1] // LANES, shift, out, opened)


def pack_small(shears, steps, small):
    small[...] = jnp.zeros_like(small)
    small[0:1, 0:BANDS] = shears[...].astype(F32)
    small[1:2, 0:BANDS] = steps[...]


def pack_edges(cube, low, high):
    for t in range(0, cube.shape[1], 512):
        at = slice(t, t + 512)
        bands = cube[:, at].astype(F32)
        none = jnp.zeros((1, 512), F32)
        low[:, at] = jnp.concatenate([bands[0:HALO], none]).astype(BF16)
        high[:, at] = jnp.concatenate([bands[BANDS - HALO :], none]).astype(BF16)


def expand_spatial(weight, bias, band, groups, one, two):
    half = 0.5 * column_of(bias[...], CH, lambda i, l: i == l)
    parts = pieces(half)
    taps = weight.shape[1]
    depth = (taps + 1) * CH
    spread = (iota((taps, depth), 1) // CH == iota((taps, depth), 0)).astype(BF16)
    wide = jnp.dot(weight[...] * jnp.bfloat16(0.5), spread, preferred_element_type=F32)
    col = iota((CH, depth), 1)
    bias_row = jnp.where(
        col == taps * CH,
        parts[0],
        jnp.where(col == taps * CH + 1, parts[1], jnp.where(col == taps * CH + 2, parts[2], 0.0)),
    )
    in_taps = col < taps * CH
    slot = col & (CH - 1)

    def block(wanted):
        return jnp.where(in_taps, jnp.where(slot == wanted, wide, 0.0), bias_row)

    for b in range(CH):
        one[b * CH : (b + 1) * CH, :] = block(b).astype(BF16)
    slots = [0, 1, 2, 3, 4, 5, 8, 9, 10, 12, 13, 14]
    for n, s in enumerate(slots):
        value = block(s)
        if 8 <= s < 12:
            value = jnp.where(band > 0, value, 0.0)
        if s >= 12:
            value = jnp.where(band < groups - 1, value, 0.0)
        two[n * CH : (n + 1) * CH, :] = value.astype(BF16)


def expand_spectral(weight, bias, out):
    depth = out.shape[1]
    rows = 24
    half = 0.5 * column_of(bias[...], CH, lambda i, l: i == l)
    parts = pieces(half)
    spread = ((iota((CH, depth), 1) & (CH - 1)) == iota((CH, depth), 0)).astype(BF16)
    wide = jnp.dot(weight[...] * jnp.bfloat16(0.5), spread, preferred_element_type=F32)
    col = iota((rows, depth), 1)
    slot = col >> 4
    place = jnp.where(slot < BANDS, slot + HALO, jnp.where(slot < BANDS + HALO, slot - BANDS, slot))
    band = iota((rows, depth), 0)
    tap = jnp.where((slot < SLOTS) & (band < BANDS), place - band, -1)
    taps = weight.shape[0] // CH
    for k in range(CH):
        block = jnp.where(col == ACT, parts[0][k : k + 1], 0.0)
        block = jnp.where(col == ACT + 1, parts[1][k : k + 1], block)
        block = jnp.where(col == ACT + 2, parts[2][k : k + 1], block)
        for d in range(taps):
            block = jnp.where(tap == d, wide[d * CH + k : d * CH + k + 1], block)
        out[k * rows : (k + 1) * rows, :] = block.astype(BF16)


def slot_vectors(smalls):
    own, below, above = (s[...] for s in smalls)

    def column(n):
        return (
            column_of(own[n : n + 1], 32, lambda i, l: (i == l) & (i < BANDS))
            + column_of(below[n : n + 1], 32, lambda i, l: (i - 24 + BANDS - HALO == l) & (i >= 24) & (i < 24 + HALO))
            + column_of(above[n : n + 1], 32, lambda i, l: (i - 28 == l) & (i >= 28) & (i < 28 + HALO))
        )

    shift = column(0).astype(jnp.int32)
    step = jnp.broadcast_to(column(1), (32, LANES))
    lane = iota((32, LANES), 1)
    within = jnp.broadcast_to(shift & (LANES - 1), (32, LANES))
    index = (lane + within) & (LANES - 1)
    steps = (shift >> 7) + jnp.where(lane + within >= LANES, 1, 0)
    return index, steps, step


def refresh(cube, aperture, edges, residual, vectors, inside, upd):
    width = cube.shape[1]
    index, steps, step = vectors
    is0, is1, is2 = steps == 0, steps == 1, steps == 2
    margin = jnp.zeros((32, LANES), BF16)
    upd[:, 0:LANES] = margin
    upd[:, LANES + width : 2 * LANES + width] = margin

    def pull(t):
        at = pl.ds(pl.multiple_of(t * LANES, LANES), LANES)
        return gather_lanes(jnp.broadcast_to(residual[:, at], (32, LANES)), index)

    def tile(t, carry):
        p0, p1, p2 = carry
        p3 = pull(t + 3)
        at = pl.ds(pl.multiple_of(t * LANES, LANES), LANES)
        pulled = jnp.where(is0, p0, jnp.where(is1, p1, jnp.where(is2, p2, p3)))
        cubes = jnp.concatenate(
            [
                cube[:, at].astype(F32),
                jnp.zeros((2, LANES), F32),
                edges[0, :, at].astype(F32),
                edges[1, :, at].astype(F32),
            ]
        )
        new = cubes + pulled * aperture[:, at].astype(F32) * step
        if inside is not None:
            new = jnp.where(inside, new, 0.0)
        upd[:, pl.ds(pl.multiple_of(t * LANES + LANES, LANES), LANES)] = new.astype(BF16)
        return p1, p2, p3

    lax.fori_loop(0, width // LANES, tile, (pull(0), pull(1), pull(2)), unroll=4)


def denoise(upd, one, two, spectral, out_weight, actives, out):
    width = out.shape[1]
    count = width // TILE
    ones = jnp.ones((CH, TILE), BF16)
    for active in actives:
        active[ACT:, :] = ones
    project_out = column_of(out_weight[...], CH, lambda i, l: i == l)

    def spatial(t, active):
        start = pl.multiple_of(t * TILE, TILE)
        window = [upd[i, :, pl.ds(start, TILE + 2 * LANES)] for i in range(3)]
        shifted = [window[i][:, LANES - 1 + j : LANES - 1 + j + TILE] for i in range(3) for j in range(3)]
        for weight, group, at in ((one, slice(0, 16), 0), (two, slice(16, 32), 16 * CH)):
            patch = jnp.concatenate([s[group] for s in shifted] + [ones])
            half = jnp.dot(weight[...], patch, preferred_element_type=F32)
            active[at : at + half.shape[0], :] = (half * jnp.tanh(half) + half).astype(BF16)

    def rest(t, active):
        start = pl.multiple_of(t * TILE, TILE)
        half = jnp.dot(spectral[...], active[...], preferred_element_type=F32)
        total = upd[1, 0:24, pl.ds(pl.multiple_of(start + LANES, LANES), TILE)].astype(F32)
        for k in range(CH):
            h = half[k * 24 : (k + 1) * 24]
            total = total + project_out[k : k + 1] * (h * jnp.tanh(h) + h)
        out[:, pl.ds(start, TILE)] = total[0:BANDS].astype(BF16)

    first, second = actives
    spatial(0, first)

    def pair(p, carry):
        spatial(2 * p + 1, second)
        rest(2 * p, first)
        spatial(2 * p + 2, first)
        rest(2 * p + 1, second)
        return carry

    lax.fori_loop(0, count // 2 - 1, pair, 0)
    spatial(count - 1, second)
    rest(count - 2, first)
    rest(count - 1, second)


def whole_kernel(
    sizes,
    cube, aperture, meas, shears, steps, sw, sb, pw, pb, ow, out,
    part, low, high, small, parts, smalls, cube_up, cube_down, ap_up, ap_down, edges, res, res_up, res_down, counts,
    one, two, spectral, upd, act_a, act_b, send, recv,
):
    groups, nrow, ncol = sizes
    band, row, col = lax.axis_index("band"), lax.axis_index("row"), lax.axis_index("col")
    last = nrow * ncol - 1
    flat = row * ncol + col
    not_first, not_last = flat > 0, flat < last

    def device(db, dr):
        r = jnp.clip(flat + dr, 0, last)
        return (lax.rem(band + db + groups, groups), r // ncol, lax.rem(r, ncol))

    barrier = pltpu.get_barrier_semaphore()

    def greet(db, dr):
        pl.semaphore_signal(barrier, inc=1, device_id=device(db, dr), device_id_type=MESH)

    for db in (1, 2, -1):
        greet(db, 0)

    @pl.when(not_first)
    def _():
        greet(0, -1)

    @pl.when(not_last)
    def _():
        greet(0, 1)

    pack_small(shears, steps, small)
    pack_edges(cube, low, high)
    project(cube, aperture, shears, part)

    pl.semaphore_wait(barrier, 3 + not_first.astype(jnp.int32) + not_last.astype(jnp.int32))
    used = [0]

    def copy(src, dst, peer):
        n = used[0]
        used[0] += 1
        return pltpu.make_async_remote_copy(
            src_ref=src, dst_ref=dst, send_sem=send.at[n], recv_sem=recv.at[n],
            device_id=device(*peer), device_id_type=MESH,
        )

    down, up = (0, 1), (0, -1)
    tiny = [copy(small, smalls.at[n], (db, 0)) for n, db in enumerate((1, -1, 2))]
    partial = [copy(part, parts.at[n], (db, 0)) for n, db in enumerate((1, -1, 2))]
    edge = [copy(high, edges.at[1, 0], (1, 0)), copy(low, edges.at[1, 1], (-1, 0))]
    to_down = [copy(aperture, ap_up, down), copy(cube, cube_up, down)]
    to_up = [copy(aperture, ap_down, up), copy(cube, cube_down, up)]
    relay_down, relay_up = copy(edges.at[1], edges.at[0], down), copy(edges.at[1], edges.at[2], up)
    res_to_down, res_to_up = copy(res, res_up, down), copy(res, res_down, up)

    for c in tiny + partial + edge:
        c.start()

    @pl.when(not_last)
    def _():
        for c in to_down:
            c.start()

    @pl.when(not_first)
    def _():
        for c in to_up:
            c.start()

    expand_spatial(sw, sb, band, groups, one, two)
    expand_spectral(pw, pb, spectral)
    for c in edge:
        c.wait_recv()

    @pl.when(not_last)
    def _():
        relay_down.start()

    @pl.when(not_first)
    def _():
        relay_up.start()

    for c in tiny:
        c.wait_recv()
    count_open(aperture, [small, smalls.at[0], smalls.at[1], smalls.at[2]], counts)
    for c in partial:
        c.wait_recv()
    width = meas.shape[1]
    predicted = part[...] + (parts[0] + parts[1] + parts[2])
    tail = width // LANES * LANES
    res[:, tail:] = jnp.zeros((1, res.shape[1] - tail), F32)
    res[:, 0:width] = (meas[...] - predicted[:, 0:width]) / jnp.maximum(counts[:, 0:width], 1.0)

    @pl.when(not_last)
    def _():
        res_to_down.start()

    @pl.when(not_first)
    def _():
        res_to_up.start()

    vectors = slot_vectors((small, smalls.at[0], smalls.at[1]))
    refresh(cube, aperture, edges.at[1], res, vectors, None, upd.at[1])

    @pl.when(not_first)
    def _():
        for c in to_down + [relay_down, res_to_down]:
            c.wait_recv()
        refresh(cube_up, ap_up, edges.at[0], res_up, vectors, None, upd.at[0])

    @pl.when(jnp.logical_not(not_first))
    def _():
        upd[0] = jnp.zeros(upd.shape[1:], BF16)

    @pl.when(not_last)
    def _():
        for c in to_up + [relay_up, res_to_up]:
            c.wait_recv()
        refresh(cube_down, ap_down, edges.at[2], res_down, vectors, None, upd.at[2])

    @pl.when(jnp.logical_not(not_last))
    def _():
        upd[2] = jnp.zeros(upd.shape[1:], BF16)

    denoise(upd, one, two, spectral, ow, (act_a, act_b), out)
    for c in tiny + partial + edge:
        c.wait_send()

    @pl.when(not_last)
    def _():
        for c in to_down + [relay_down, res_to_down]:
            c.wait_send()

    @pl.when(not_first)
    def _():
        for c in to_up + [relay_up, res_to_up]:
            c.wait_send()


def solution(mesh):
    sizes = tuple(mesh.shape[a] for a in ("band", "row", "col"))
    vmem = pl.BlockSpec(memory_space=pltpu.VMEM)

    def on_device(cube, aperture, meas, shears, steps, sw, sb, pw, pb, ow):
        width = cube.shape[2]
        cube = cube.reshape(cube.shape[0], width)
        shears, steps, sb, pb, ow = (a.reshape(1, -1) for a in (shears, steps, sb, pb, ow))
        pw = pw.reshape(-1, CH)
        wide = (meas.shape[1] + 2 * LANES - 1) // LANES * LANES
        line = pltpu.VMEM((1, wide), F32)
        out = pl.pallas_call(
            lambda *r: whole_kernel(sizes, *r),
            name="whole",
            out_shape=jax.ShapeDtypeStruct(cube.shape, BF16),
            in_specs=[vmem] * 10,
            out_specs=vmem,
            scratch_shapes=[
                line,
                pltpu.VMEM((4, width), BF16),
                pltpu.VMEM((4, width), BF16),
                pltpu.VMEM((8, LANES), F32),
                pltpu.VMEM((3, 1, wide), F32),
                pltpu.VMEM((3, 8, LANES), F32),
                pltpu.VMEM(cube.shape, BF16),
                pltpu.VMEM(cube.shape, BF16),
                pltpu.VMEM(aperture.shape, jnp.int32),
                pltpu.VMEM(aperture.shape, jnp.int32),
                pltpu.VMEM((3, 2, 4, width), BF16),
                line,
                line,
                line,
                line,
                pltpu.VMEM((16 * CH, 10 * CH), BF16),
                pltpu.VMEM((12 * CH, 10 * CH), BF16),
                pltpu.VMEM((24 * CH, ACT + CH), BF16),
                pltpu.VMEM((3, 32, width + 2 * LANES), BF16),
                pltpu.VMEM((ACT + CH, TILE), BF16),
                pltpu.VMEM((ACT + CH, TILE), BF16),
                pltpu.SemaphoreType.DMA((16,)),
                pltpu.SemaphoreType.DMA((16,)),
            ],
            compiler_params=pltpu.CompilerParams(collective_id=0, has_side_effects=True),
        )(cube, aperture, meas, shears, steps, sw, sb, pw, pb, ow)
        return out.reshape(out.shape[0], 1, width)

    in_specs = (
        P("band", ("row", "col"), None),
        P(("row", "col"), None),
        P(("row", "col"), None),
        P("band"),
        P("band"),
        P(),
        P(),
        P(),
        P(),
        P(),
    )
    return jax.shard_map(
        on_device, mesh=mesh, in_specs=in_specs, out_specs=P("band", ("row", "col"), None), check_vma=False
    )
```

```python
import jax
import jax.numpy as jnp
from jax import lax
from jax.experimental import pallas as pl
from jax.experimental.pallas import tpu as pltpu
from jax.sharding import PartitionSpec as P

MESH = pl.DeviceIdType.MESH
F32 = jnp.float32
BF16 = jnp.bfloat16
LANES = 128
BANDS = 22
HALO = 3
CH = 16
SLOTS = 28
ACT = SLOTS * CH
TILE = 256


def iota(shape, dim):
    return lax.broadcasted_iota(jnp.int32, shape, dim)


def column_of(row, rows, where):
    shape = (rows, row.shape[1])
    return jnp.sum(
        jnp.where(where(iota(shape, 0), iota(shape, 1)), row, 0.0), axis=1, keepdims=True
    )


def pieces(x):
    high = x.astype(BF16).astype(F32)
    middle = (x - high).astype(BF16).astype(F32)
    return high, middle, x - high - middle


def gather_lanes(x, index):
    return jnp.take_along_axis(x, index, axis=1, mode="promise_in_bounds")


def place(tiles, row, acc, tile_of, add):
    shift = column_of(row, 24, lambda i, l: i == l).astype(jnp.int32)
    lane = iota((24, LANES), 1)
    within = jnp.broadcast_to(shift & (LANES - 1), (24, LANES))
    index = (lane - within) & (LANES - 1)
    steps = (shift >> 7) + jnp.where(lane < within, 1, 0)
    is0, is1, is2 = steps == 0, steps == 1, steps == 2
    none = jnp.zeros((24, LANES), F32)
    turned = []
    for t in range(acc.shape[1] // LANES):
        at = slice(t * LANES, (t + 1) * LANES)
        turned.append(gather_lanes(tile_of(t), index) if t < tiles else none)
        back = [turned[t - e] if t >= e else none for e in range(4)]
        here = jnp.where(is0, back[0], jnp.where(is1, back[1], jnp.where(is2, back[2], back[3])))
        total = here[0:8] + here[8:16] + here[16:24]
        acc[:, at] = acc[:, at] + total if add else total


def collapse(acc, out):
    out[...] = jnp.sum(acc[...], axis=0, keepdims=True)


def project(cube, aperture, shears, acc):
    def masked(t):
        at = slice(t * LANES, (t + 1) * LANES)
        bands = jnp.concatenate([cube[:, at].astype(F32), jnp.zeros((24 - BANDS, LANES), F32)])
        return bands * aperture[:, at].astype(F32)

    place(cube.shape[1] // LANES, shears[...].astype(F32), acc, masked, False)


def count_open(aperture, small, acc, add):
    own = iota((24, LANES), 0) < BANDS

    def opened(t):
        open_t = aperture[:, t * LANES : (t + 1) * LANES].astype(F32)
        return jnp.where(own, jnp.broadcast_to(open_t, (24, LANES)), 0.0)

    place(aperture.shape[1] // LANES, small[0:1], acc, opened, add)


def pack_small(shears, steps, small):
    small[...] = jnp.zeros_like(small)
    small[0:1, 0:BANDS] = shears[...].astype(F32)
    small[1:2, 0:BANDS] = steps[...]


def pack_edges(cube, low, high):
    for t in range(0, cube.shape[1], 512):
        at = slice(t, t + 512)
        bands = cube[:, at].astype(F32)
        none = jnp.zeros((1, 512), F32)
        low[:, at] = jnp.concatenate([bands[0:HALO], none]).astype(BF16)
        high[:, at] = jnp.concatenate([bands[BANDS - HALO :], none]).astype(BF16)


def expand_spatial(weight, bias, band, groups, one, two):
    half = 0.5 * column_of(bias[...], CH, lambda i, l: i == l)
    parts = pieces(half)
    taps = weight.shape[1]
    depth = (taps + 1) * CH
    spread = (iota((taps, depth), 1) // CH == iota((taps, depth), 0)).astype(BF16)
    wide = jnp.dot(weight[...] * jnp.bfloat16(0.5), spread, preferred_element_type=F32)
    col = iota((CH, depth), 1)
    bias_row = jnp.where(
        col == taps * CH,
        parts[0],
        jnp.where(col == taps * CH + 1, parts[1], jnp.where(col == taps * CH + 2, parts[2], 0.0)),
    )
    in_taps = col < taps * CH
    slot = col & (CH - 1)

    def block(wanted):
        return jnp.where(in_taps, jnp.where(slot == wanted, wide, 0.0), bias_row)

    for b in range(CH):
        one[b * CH : (b + 1) * CH, :] = block(b).astype(BF16)
    slots = [0, 1, 2, 3, 4, 5, 8, 9, 10, 12, 13, 14]
    for n, s in enumerate(slots):
        value = block(s)
        if 8 <= s < 12:
            value = jnp.where(band > 0, value, 0.0)
        if s >= 12:
            value = jnp.where(band < groups - 1, value, 0.0)
        two[n * CH : (n + 1) * CH, :] = value.astype(BF16)


def expand_spectral(weight, bias, out):
    depth = out.shape[1]
    rows = 8
    half = 0.5 * column_of(bias[...], CH, lambda i, l: i == l)
    parts = pieces(half)
    spread = ((iota((CH, depth), 1) & (CH - 1)) == iota((CH, depth), 0)).astype(BF16)
    wide = jnp.dot(weight[...] * jnp.bfloat16(0.5), spread, preferred_element_type=F32)
    col = iota((rows, depth), 1)
    start = depth - CH
    tap = jnp.where(col < start, (col >> 4) - iota((rows, depth), 0), -1)
    taps = weight.shape[0] // CH
    for k in range(CH):
        block = jnp.where(col == start, parts[0][k : k + 1], 0.0)
        block = jnp.where(col == start + 1, parts[1][k : k + 1], block)
        block = jnp.where(col == start + 2, parts[2][k : k + 1], block)
        for d in range(taps):
            block = jnp.where(tap == d, wide[d * CH + k : d * CH + k + 1], block)
        out[k * rows : (k + 1) * rows, :] = block.astype(BF16)


def slot_vectors(smalls):
    own, below, above = (s[...] for s in smalls)

    def column(n):
        return (
            column_of(own[n : n + 1], 32, lambda i, l: (i == l) & (i < BANDS))
            + column_of(below[n : n + 1], 32, lambda i, l: (i - 24 + BANDS - HALO == l) & (i >= 24) & (i < 24 + HALO))
            + column_of(above[n : n + 1], 32, lambda i, l: (i - 28 == l) & (i >= 28) & (i < 28 + HALO))
        )

    shift = column(0).astype(jnp.int32)
    step = jnp.broadcast_to(column(1), (32, LANES))
    lane = iota((32, LANES), 1)
    within = jnp.broadcast_to(shift & (LANES - 1), (32, LANES))
    index = (lane + within) & (LANES - 1)
    steps = (shift >> 7) + jnp.where(lane + within >= LANES, 1, 0)
    return index, steps, step


def refresh(cube, aperture, edges, residual, vectors, upd):
    width = cube.shape[1]
    tiles = width // LANES
    index, steps, step = vectors
    is0, is1, is2 = steps == 0, steps == 1, steps == 2
    lane = iota((32, LANES), 1)
    leftmost, rightmost = lane == 0, lane == LANES - 1
    none = jnp.zeros((32, LANES), F32)

    def pull(t):
        at = pl.ds(pl.multiple_of(t * LANES, LANES), LANES)
        return gather_lanes(jnp.broadcast_to(residual[:, at], (32, LANES)), index)

    def tile(t, carry):
        p0, p1, p2, before, after = carry
        p3 = pull(t + 3)
        at = pl.ds(pl.multiple_of(t * LANES, LANES), LANES)
        pulled = jnp.where(is0, p0, jnp.where(is1, p1, jnp.where(is2, p2, p3)))
        cubes = jnp.concatenate(
            [
                cube[:, at].astype(F32),
                jnp.zeros((2, LANES), F32),
                edges[0, :, at].astype(F32),
                edges[1, :, at].astype(F32),
            ]
        )
        new = cubes + pulled * aperture[:, at].astype(F32) * step
        up, down = pltpu.roll(new, 1, 1), pltpu.roll(new, LANES - 1, 1)
        upd[0, :, at] = jnp.where(leftmost, before, up).astype(BF16)
        upd[1, :, at] = new.astype(BF16)
        upd[2, :, at] = jnp.where(rightmost, down, after).astype(BF16)
        return p1, p2, p3, up, down

    last = lax.fori_loop(0, tiles, tile, (pull(0), pull(1), pull(2), none, none), unroll=4)
    upd[2, :, tiles * LANES : (tiles + 1) * LANES] = jnp.where(rightmost, 0.0, last[4]).astype(BF16)


def denoise(upd, one, two, spectral, out_weight, active, out):
    width = out.shape[1]
    count = width // TILE
    ones = jnp.ones((CH, TILE), BF16)
    active[ACT:, :] = jnp.zeros((active.shape[0] - ACT, TILE), BF16)
    weights = column_of(out_weight[...], CH, lambda i, l: i == l)
    own = HALO * CH

    def spatial(t):
        start = pl.multiple_of(t * TILE, TILE)
        shifted = [upd[i, j, :, pl.ds(pl.multiple_of(start + j // 2 * LANES, LANES), TILE)] for i in range(3) for j in range(3)]
        halves = []
        for weight, group in ((one, slice(0, 16)), (two, slice(16, 32))):
            patch = jnp.concatenate([s[group] for s in shifted] + [ones])
            half = jnp.dot(weight[...], patch, preferred_element_type=F32)
            halves.append((half * jnp.tanh(half) + half).astype(BF16))
        first, second = halves
        top = own + first.shape[0]
        edge = second.shape[0] - 2 * own
        active[own:top, :] = first
        active[top : top + edge, :] = second[0:edge]
        active[0:own, :] = second[edge : edge + own]
        active[top + edge : ACT, :] = second[edge + own :]

    def rest(t):
        start = pl.multiple_of(t * TILE, TILE)
        centre = upd[1, 1, 0:24, pl.ds(start, TILE)].astype(F32)
        totals = []
        for g in range(3):
            source = jnp.concatenate([active[g * 8 * CH : (g * 8 + 14) * CH, :], ones])
            half = jnp.dot(spectral[...], source, preferred_element_type=F32)
            total = centre[g * 8 : (g + 1) * 8]
            for k in range(CH):
                h = half[k * 8 : (k + 1) * 8]
                total = total + weights[k : k + 1] * (h * jnp.tanh(h) + h)
            totals.append(total)
        out[:, pl.ds(start, TILE)] = jnp.concatenate(totals)[0:BANDS].astype(BF16)

    spatial(0)

    def body(t, carry):
        rest(t)
        spatial(t + 1)
        return carry

    lax.fori_loop(0, count - 1, body, 0)
    rest(count - 1)


def whole_kernel(
    sizes,
    cube, aperture, meas, shears, steps, sw, sb, pw, pb, ow, out,
    part, low, high, small, parts, smalls, cube_up, cube_down, ap_up, ap_down, edges, res, res_up, res_down, acc, counts,
    one, two, spectral, upd, active, send, recv,
):
    groups, nrow, ncol = sizes
    band, row, col = lax.axis_index("band"), lax.axis_index("row"), lax.axis_index("col")
    last = nrow * ncol - 1
    flat = row * ncol + col
    not_first, not_last = flat > 0, flat < last

    def device(db, dr):
        r = jnp.clip(flat + dr, 0, last)
        return (lax.rem(band + db + groups, groups), r // ncol, lax.rem(r, ncol))

    barrier = pltpu.get_barrier_semaphore()

    def greet(db, dr):
        pl.semaphore_signal(barrier, inc=1, device_id=device(db, dr), device_id_type=MESH)

    for db in (1, 2, -1):
        greet(db, 0)

    @pl.when(not_first)
    def _():
        greet(0, -1)

    @pl.when(not_last)
    def _():
        greet(0, 1)

    pack_small(shears, steps, small)
    pack_edges(cube, low, high)
    pl.semaphore_wait(barrier, 3 + not_first.astype(jnp.int32) + not_last.astype(jnp.int32))
    used = [0]

    def copy(src, dst, peer):
        n = used[0]
        used[0] += 1
        return pltpu.make_async_remote_copy(
            src_ref=src, dst_ref=dst, send_sem=send.at[n], recv_sem=recv.at[n],
            device_id=device(*peer), device_id_type=MESH,
        )

    down, up = (0, 1), (0, -1)
    tiny = [copy(small, smalls.at[n], (db, 0)) for n, db in enumerate((1, -1, 2))]
    partial = [copy(part, parts.at[n], (db, 0)) for n, db in enumerate((1, -1, 2))]
    edge = [copy(high, edges.at[1, 0], (1, 0)), copy(low, edges.at[1, 1], (-1, 0))]
    to_down = [copy(aperture, ap_up, down), copy(cube, cube_up, down)]
    to_up = [copy(aperture, ap_down, up), copy(cube, cube_down, up)]
    relay_down, relay_up = copy(edges.at[1], edges.at[0], down), copy(edges.at[1], edges.at[2], up)
    res_to_down, res_to_up = copy(res, res_up, down), copy(res, res_down, up)

    for c in tiny + edge:
        c.start()
    project(cube, aperture, shears, acc)
    collapse(acc, part)
    for c in partial:
        c.start()

    @pl.when(not_last)
    def _():
        for c in to_down:
            c.start()

    @pl.when(not_first)
    def _():
        for c in to_up:
            c.start()

    expand_spectral(pw, pb, spectral)
    for c in edge:
        c.wait_recv()

    @pl.when(not_last)
    def _():
        relay_down.start()

    @pl.when(not_first)
    def _():
        relay_up.start()

    expand_spatial(sw, sb, band, groups, one, two)
    count_open(aperture, small, acc, False)
    for c in tiny:
        c.wait_recv()
    for n in range(3):
        count_open(aperture, smalls.at[n], acc, True)
    collapse(acc, counts)
    for c in partial:
        c.wait_recv()
    width = meas.shape[1]
    predicted = part[...] + (parts[0] + parts[1] + parts[2])
    tail = width // LANES * LANES
    res[:, tail:] = jnp.zeros((1, res.shape[1] - tail), F32)
    res[:, 0:width] = (meas[...] - predicted[:, 0:width]) / jnp.maximum(counts[:, 0:width], 1.0)

    @pl.when(not_last)
    def _():
        res_to_down.start()

    @pl.when(not_first)
    def _():
        res_to_up.start()

    vectors = slot_vectors((small, smalls.at[0], smalls.at[1]))
    refresh(cube, aperture, edges.at[1], res, vectors, upd.at[1])

    @pl.when(not_first)
    def _():
        for c in to_down + [relay_down, res_to_down]:
            c.wait_recv()
        refresh(cube_up, ap_up, edges.at[0], res_up, vectors, upd.at[0])

    @pl.when(jnp.logical_not(not_first))
    def _():
        upd[0] = jnp.zeros(upd.shape[1:], BF16)

    @pl.when(not_last)
    def _():
        for c in to_up + [relay_up, res_to_up]:
            c.wait_recv()
        refresh(cube_down, ap_down, edges.at[2], res_down, vectors, upd.at[2])

    @pl.when(jnp.logical_not(not_last))
    def _():
        upd[2] = jnp.zeros(upd.shape[1:], BF16)

    denoise(upd, one, two, spectral, ow, active, out)
    for c in tiny + partial + edge:
        c.wait_send()

    @pl.when(not_last)
    def _():
        for c in to_down + [relay_down, res_to_down]:
            c.wait_send()

    @pl.when(not_first)
    def _():
        for c in to_up + [relay_up, res_to_up]:
            c.wait_send()


def solution(mesh):
    sizes = tuple(mesh.shape[a] for a in ("band", "row", "col"))
    vmem = pl.BlockSpec(memory_space=pltpu.VMEM)

    def on_device(cube, aperture, meas, shears, steps, sw, sb, pw, pb, ow):
        width = cube.shape[2]
        cube = cube.reshape(cube.shape[0], width)
        shears, steps, sb, pb, ow = (a.reshape(1, -1) for a in (shears, steps, sb, pb, ow))
        pw = pw.reshape(-1, CH)
        wide = (meas.shape[1] + 2 * LANES - 1) // LANES * LANES
        line = pltpu.VMEM((1, wide), F32)
        out = pl.pallas_call(
            lambda *r: whole_kernel(sizes, *r),
            name="whole",
            out_shape=jax.ShapeDtypeStruct(cube.shape, BF16),
            in_specs=[vmem] * 10,
            out_specs=vmem,
            scratch_shapes=[
                line,
                pltpu.VMEM((4, width), BF16),
                pltpu.VMEM((4, width), BF16),
                pltpu.VMEM((8, LANES), F32),
                pltpu.VMEM((3, 1, wide), F32),
                pltpu.VMEM((3, 8, LANES), F32),
                pltpu.VMEM(cube.shape, BF16),
                pltpu.VMEM(cube.shape, BF16),
                pltpu.VMEM(aperture.shape, jnp.int32),
                pltpu.VMEM(aperture.shape, jnp.int32),
                pltpu.VMEM((3, 2, 4, width), BF16),
                line,
                line,
                line,
                pltpu.VMEM((8, wide), F32),
                line,
                pltpu.VMEM((16 * CH, 10 * CH), BF16),
                pltpu.VMEM((12 * CH, 10 * CH), BF16),
                pltpu.VMEM((8 * CH, 15 * CH), BF16),
                pltpu.VMEM((3, 3, 32, width + LANES), BF16),
                pltpu.VMEM((ACT + 2 * CH, TILE), BF16),
                pltpu.SemaphoreType.DMA((16,)),
                pltpu.SemaphoreType.DMA((16,)),
            ],
            compiler_params=pltpu.CompilerParams(collective_id=0, has_side_effects=True),
        )(cube, aperture, meas, shears, steps, sw, sb, pw, pb, ow)
        return out.reshape(out.shape[0], 1, width)

    in_specs = (
        P("band", ("row", "col"), None),
        P(("row", "col"), None),
        P(("row", "col"), None),
        P("band"),
        P("band"),
        P(),
        P(),
        P(),
        P(),
        P(),
    )
    return jax.shard_map(
        on_device, mesh=mesh, in_specs=in_specs, out_specs=P("band", ("row", "col"), None), check_vma=False
    )
```

```python
import jax
import jax.numpy as jnp
from jax import lax
from jax.experimental import pallas as pl
from jax.experimental.pallas import tpu as pltpu
from jax.sharding import PartitionSpec as P

MESH = pl.DeviceIdType.MESH
F32 = jnp.float32
BF16 = jnp.bfloat16
LANES = 128
BANDS = 22
HALO = 3
CH = 16
SLOTS = 28
ACT = SLOTS * CH
TILE = 256


def iota(shape, dim):
    return lax.broadcasted_iota(jnp.int32, shape, dim)


def column_of(row, rows, where):
    shape = (rows, row.shape[1])
    return jnp.sum(
        jnp.where(where(iota(shape, 0), iota(shape, 1)), row, 0.0), axis=1, keepdims=True
    )


def pieces(x):
    high = x.astype(BF16).astype(F32)
    middle = (x - high).astype(BF16).astype(F32)
    return high, middle, x - high - middle


def gather_lanes(x, index):
    return jnp.take_along_axis(x, index, axis=1, mode="promise_in_bounds")


def place(tiles, row, acc, tile_of, add):
    shift = column_of(row, 24, lambda i, l: i == l).astype(jnp.int32)
    lane = iota((24, LANES), 1)
    within = jnp.broadcast_to(shift & (LANES - 1), (24, LANES))
    index = (lane - within) & (LANES - 1)
    steps = (shift >> 7) + jnp.where(lane < within, 1, 0)
    is0, is1, is2 = steps == 0, steps == 1, steps == 2
    none = jnp.zeros((24, LANES), F32)
    turned = []
    for t in range(acc.shape[1] // LANES):
        at = slice(t * LANES, (t + 1) * LANES)
        turned.append(gather_lanes(tile_of(t), index) if t < tiles else none)
        back = [turned[t - e] if t >= e else none for e in range(4)]
        here = jnp.where(is0, back[0], jnp.where(is1, back[1], jnp.where(is2, back[2], back[3])))
        total = here[0:8] + here[8:16] + here[16:24]
        acc[:, at] = acc[:, at] + total if add else total


def collapse(acc, out):
    out[...] = jnp.sum(acc[...], axis=0, keepdims=True)


def project(cube, aperture, shears, acc):
    def masked(t):
        at = slice(t * LANES, (t + 1) * LANES)
        bands = jnp.concatenate([cube[:, at].astype(F32), jnp.zeros((24 - BANDS, LANES), F32)])
        return bands * aperture[:, at].astype(F32)

    place(cube.shape[1] // LANES, shears[...].astype(F32), acc, masked, False)


def count_open(aperture, small, acc, add):
    own = iota((24, LANES), 0) < BANDS

    def opened(t):
        open_t = aperture[:, t * LANES : (t + 1) * LANES].astype(F32)
        return jnp.where(own, jnp.broadcast_to(open_t, (24, LANES)), 0.0)

    place(aperture.shape[1] // LANES, small[0:1], acc, opened, add)


def pack_small(shears, steps, small):
    small[...] = jnp.zeros_like(small)
    small[0:1, 0:BANDS] = shears[...].astype(F32)
    small[1:2, 0:BANDS] = steps[...]


def pack_edges(cube, low, high):
    for t in range(0, cube.shape[1], 512):
        at = slice(t, t + 512)
        bands = cube[:, at].astype(F32)
        none = jnp.zeros((1, 512), F32)
        low[:, at] = jnp.concatenate([bands[0:HALO], none]).astype(BF16)
        high[:, at] = jnp.concatenate([bands[BANDS - HALO :], none]).astype(BF16)


def expand_spatial(weight, bias, band, groups, one, two):
    half = 0.5 * column_of(bias[...], CH, lambda i, l: i == l)
    parts = pieces(half)
    taps = weight.shape[1]
    depth = (taps + 1) * CH
    spread = (iota((taps, depth), 1) // CH == iota((taps, depth), 0)).astype(BF16)
    wide = jnp.dot(weight[...] * jnp.bfloat16(0.5), spread, preferred_element_type=F32)
    col = iota((CH, depth), 1)
    bias_row = jnp.where(
        col == taps * CH,
        parts[0],
        jnp.where(col == taps * CH + 1, parts[1], jnp.where(col == taps * CH + 2, parts[2], 0.0)),
    )
    in_taps = col < taps * CH
    slot = col & (CH - 1)

    def block(wanted):
        return jnp.where(in_taps, jnp.where(slot == wanted, wide, 0.0), bias_row)

    for b in range(CH):
        one[b * CH : (b + 1) * CH, :] = block(b).astype(BF16)
    slots = [0, 1, 2, 3, 4, 5, 8, 9, 10, 12, 13, 14]
    for n, s in enumerate(slots):
        value = block(s)
        if 8 <= s < 12:
            value = jnp.where(band > 0, value, 0.0)
        if s >= 12:
            value = jnp.where(band < groups - 1, value, 0.0)
        two[n * CH : (n + 1) * CH, :] = value.astype(BF16)


def expand_spectral(weight, bias, out):
    depth = out.shape[1]
    rows = 8
    half = 0.5 * column_of(bias[...], CH, lambda i, l: i == l)
    parts = pieces(half)
    spread = ((iota((CH, depth), 1) & (CH - 1)) == iota((CH, depth), 0)).astype(BF16)
    wide = jnp.dot(weight[...] * jnp.bfloat16(0.5), spread, preferred_element_type=F32)
    col = iota((rows, depth), 1)
    start = depth - CH
    tap = jnp.where(col < start, (col >> 4) - iota((rows, depth), 0), -1)
    taps = weight.shape[0] // CH
    for k in range(CH):
        block = jnp.where(col == start, parts[0][k : k + 1], 0.0)
        block = jnp.where(col == start + 1, parts[1][k : k + 1], block)
        block = jnp.where(col == start + 2, parts[2][k : k + 1], block)
        for d in range(taps):
            block = jnp.where(tap == d, wide[d * CH + k : d * CH + k + 1], block)
        out[k * rows : (k + 1) * rows, :] = block.astype(BF16)


def slot_vectors(smalls):
    own, below, above = (s[...] for s in smalls)

    def column(n):
        return (
            column_of(own[n : n + 1], 32, lambda i, l: (i == l) & (i < BANDS))
            + column_of(below[n : n + 1], 32, lambda i, l: (i - 24 + BANDS - HALO == l) & (i >= 24) & (i < 24 + HALO))
            + column_of(above[n : n + 1], 32, lambda i, l: (i - 28 == l) & (i >= 28) & (i < 28 + HALO))
        )

    shift = column(0).astype(jnp.int32)
    step = jnp.broadcast_to(column(1), (32, LANES))
    lane = iota((32, LANES), 1)
    within = jnp.broadcast_to(shift & (LANES - 1), (32, LANES))
    index = (lane + within) & (LANES - 1)
    steps = (shift >> 7) + jnp.where(lane + within >= LANES, 1, 0)
    return index, steps, step


def refresh(cube, aperture, edges, residual, vectors, upd):
    width = cube.shape[1]
    tiles = width // LANES
    index, steps, step = vectors
    is0, is1, is2 = steps == 0, steps == 1, steps == 2
    lane = iota((32, LANES), 1)
    leftmost, rightmost = lane == 0, lane == LANES - 1
    none = jnp.zeros((32, LANES), F32)

    def pull(t):
        at = pl.ds(pl.multiple_of(t * LANES, LANES), LANES)
        return gather_lanes(jnp.broadcast_to(residual[:, at], (32, LANES)), index)

    def tile(t, carry):
        p0, p1, p2, before, after = carry
        p3 = pull(t + 3)
        at = pl.ds(pl.multiple_of(t * LANES, LANES), LANES)
        pulled = jnp.where(is0, p0, jnp.where(is1, p1, jnp.where(is2, p2, p3)))
        cubes = jnp.concatenate(
            [
                cube[:, at].astype(F32),
                jnp.zeros((2, LANES), F32),
                edges[0, :, at].astype(F32),
                edges[1, :, at].astype(F32),
            ]
        )
        new = cubes + pulled * aperture[:, at].astype(F32) * step
        up, down = pltpu.roll(new, 1, 1), pltpu.roll(new, LANES - 1, 1)
        upd[0, :, at] = jnp.where(leftmost, before, up).astype(BF16)
        upd[1, :, at] = new.astype(BF16)
        upd[2, :, at] = jnp.where(rightmost, down, after).astype(BF16)
        return p1, p2, p3, up, down

    last = lax.fori_loop(0, tiles, tile, (pull(0), pull(1), pull(2), none, none), unroll=4)
    upd[2, :, tiles * LANES : (tiles + 1) * LANES] = jnp.where(rightmost, 0.0, last[4]).astype(BF16)


def denoise(upd, one, two, spectral, out_weight, active, out):
    width = out.shape[1]
    count = width // TILE
    ones = jnp.ones((CH, TILE), BF16)
    active[ACT:, :] = jnp.zeros((active.shape[0] - ACT, TILE), BF16)
    weights = column_of(out_weight[...], CH, lambda i, l: i == l)
    own = HALO * CH

    def spatial(t):
        start = pl.multiple_of(t * TILE, TILE)
        shifted = [upd[i, j, :, pl.ds(pl.multiple_of(start + j // 2 * LANES, LANES), TILE)] for i in range(3) for j in range(3)]
        halves = []
        for weight, group in ((one, slice(0, 16)), (two, slice(16, 32))):
            patch = jnp.concatenate([s[group] for s in shifted] + [ones])
            half = jnp.dot(weight[...], patch, preferred_element_type=F32)
            halves.append((half * jnp.tanh(half) + half).astype(BF16))
        first, second = halves
        top = own + first.shape[0]
        edge = second.shape[0] - 2 * own
        active[own:top, :] = first
        active[top : top + edge, :] = second[0:edge]
        active[0:own, :] = second[edge : edge + own]
        active[top + edge : ACT, :] = second[edge + own :]

    def rest(t):
        start = pl.multiple_of(t * TILE, TILE)
        centre = upd[1, 1, 0:24, pl.ds(start, TILE)].astype(F32)
        totals = []
        for g in range(3):
            source = jnp.concatenate([active[g * 8 * CH : (g * 8 + 14) * CH, :], ones])
            half = jnp.dot(spectral[...], source, preferred_element_type=F32)
            total = centre[g * 8 : (g + 1) * 8]
            for k in range(CH):
                h = half[k * 8 : (k + 1) * 8]
                total = total + weights[k : k + 1] * (h * jnp.tanh(h) + h)
            totals.append(total)
        out[:, pl.ds(start, TILE)] = jnp.concatenate(totals)[0:BANDS].astype(BF16)

    spatial(0)

    def body(t, carry):
        rest(t)
        spatial(t + 1)
        return carry

    lax.fori_loop(0, count - 1, body, 0)
    rest(count - 1)


def whole_kernel(
    sizes,
    cube, aperture, meas, shears, steps, sw, sb, pw, pb, ow, out,
    part, low, high, small, parts, smalls, cube_up, cube_down, ap_up, ap_down, edges, res, res_up, res_down, acc, counts,
    one, two, spectral, upd, active, send, recv,
):
    groups, nrow, ncol = sizes
    band, row, col = lax.axis_index("band"), lax.axis_index("row"), lax.axis_index("col")
    last = nrow * ncol - 1
    flat = row * ncol + col
    not_first, not_last = flat > 0, flat < last

    def device(db, dr):
        r = jnp.clip(flat + dr, 0, last)
        return (lax.rem(band + db + groups, groups), r // ncol, lax.rem(r, ncol))

    barrier = pltpu.get_barrier_semaphore()

    def greet(db, dr):
        pl.semaphore_signal(barrier, inc=1, device_id=device(db, dr), device_id_type=MESH)

    for db in (1, 2, -1):
        greet(db, 0)

    @pl.when(not_first)
    def _():
        greet(0, -1)

    @pl.when(not_last)
    def _():
        greet(0, 1)

    pack_small(shears, steps, small)
    pack_edges(cube, low, high)
    pl.semaphore_wait(barrier, 3 + not_first.astype(jnp.int32) + not_last.astype(jnp.int32))
    used = [0]

    def copy(src, dst, peer):
        n = used[0]
        used[0] += 1
        return pltpu.make_async_remote_copy(
            src_ref=src, dst_ref=dst, send_sem=send.at[n], recv_sem=recv.at[n],
            device_id=device(*peer), device_id_type=MESH,
        )

    down, up = (0, 1), (0, -1)
    tiny = [copy(small, smalls.at[n], (db, 0)) for n, db in enumerate((1, -1, 2))]
    partial = [copy(part, parts.at[n], (db, 0)) for n, db in enumerate((1, -1, 2))]
    edge = [copy(high, edges.at[1, 0], (1, 0)), copy(low, edges.at[1, 1], (-1, 0))]
    to_down = [copy(aperture, ap_up, down), copy(cube, cube_up, down)]
    to_up = [copy(aperture, ap_down, up), copy(cube, cube_down, up)]
    relay_down, relay_up = copy(edges.at[1], edges.at[0], down), copy(edges.at[1], edges.at[2], up)
    res_to_down, res_to_up = copy(res, res_up, down), copy(res, res_down, up)

    for c in tiny + edge:
        c.start()
    project(cube, aperture, shears, acc)
    collapse(acc, part)
    for c in partial:
        c.start()

    @pl.when(not_last)
    def _():
        for c in to_down:
            c.start()

    @pl.when(not_first)
    def _():
        for c in to_up:
            c.start()

    expand_spectral(pw, pb, spectral)
    for c in edge:
        c.wait_recv()

    @pl.when(not_last)
    def _():
        relay_down.start()

    @pl.when(not_first)
    def _():
        relay_up.start()

    expand_spatial(sw, sb, band, groups, one, two)
    count_open(aperture, small, acc, False)
    for c in tiny:
        c.wait_recv()
    for n in range(3):
        count_open(aperture, smalls.at[n], acc, True)
    collapse(acc, counts)
    for c in partial:
        c.wait_recv()
    width = meas.shape[1]
    predicted = part[...] + (parts[0] + parts[1] + parts[2])
    tail = width // LANES * LANES
    res[:, tail:] = jnp.zeros((1, res.shape[1] - tail), F32)
    res[:, 0:width] = (meas[...] - predicted[:, 0:width]) / jnp.maximum(counts[:, 0:width], 1.0)

    @pl.when(not_last)
    def _():
        res_to_down.start()

    @pl.when(not_first)
    def _():
        res_to_up.start()

    vectors = slot_vectors((small, smalls.at[0], smalls.at[1]))
    refresh(cube, aperture, edges.at[1], res, vectors, upd.at[1])

    @pl.when(not_first)
    def _():
        for c in to_down + [relay_down, res_to_down]:
            c.wait_recv()
        refresh(cube_up, ap_up, edges.at[0], res_up, vectors, upd.at[0])

    @pl.when(jnp.logical_not(not_first))
    def _():
        upd[0] = jnp.zeros(upd.shape[1:], BF16)

    @pl.when(not_last)
    def _():
        for c in to_up + [relay_up, res_to_up]:
            c.wait_recv()
        refresh(cube_down, ap_down, edges.at[2], res_down, vectors, upd.at[2])

    @pl.when(jnp.logical_not(not_last))
    def _():
        upd[2] = jnp.zeros(upd.shape[1:], BF16)

    denoise(upd, one, two, spectral, ow, active, out)
    for c in tiny + partial + edge:
        c.wait_send()

    @pl.when(not_last)
    def _():
        for c in to_down + [relay_down, res_to_down]:
            c.wait_send()

    @pl.when(not_first)
    def _():
        for c in to_up + [relay_up, res_to_up]:
            c.wait_send()


def solution(mesh):
    sizes = tuple(mesh.shape[a] for a in ("band", "row", "col"))
    vmem = pl.BlockSpec(memory_space=pltpu.VMEM)

    def on_device(cube, aperture, meas, shears, steps, sw, sb, pw, pb, ow):
        width = cube.shape[2]
        cube = cube.reshape(cube.shape[0], width)
        shears, steps, sb, pb, ow = (a.reshape(1, -1) for a in (shears, steps, sb, pb, ow))
        pw = pw.reshape(-1, CH)
        wide = (meas.shape[1] + 2 * LANES - 1) // LANES * LANES
        line = pltpu.VMEM((1, wide), F32)
        out = pl.pallas_call(
            lambda *r: whole_kernel(sizes, *r),
            name="whole",
            out_shape=jax.ShapeDtypeStruct(cube.shape, BF16),
            in_specs=[vmem] * 10,
            out_specs=vmem,
            scratch_shapes=[
                line,
                pltpu.VMEM((4, width), BF16),
                pltpu.VMEM((4, width), BF16),
                pltpu.VMEM((8, LANES), F32),
                pltpu.VMEM((3, 1, wide), F32),
                pltpu.VMEM((3, 8, LANES), F32),
                pltpu.VMEM(cube.shape, BF16),
                pltpu.VMEM(cube.shape, BF16),
                pltpu.VMEM(aperture.shape, jnp.int32),
                pltpu.VMEM(aperture.shape, jnp.int32),
                pltpu.VMEM((3, 2, 4, width), BF16),
                line,
                line,
                line,
                pltpu.VMEM((8, wide), F32),
                line,
                pltpu.VMEM((16 * CH, 10 * CH), BF16),
                pltpu.VMEM((12 * CH, 10 * CH), BF16),
                pltpu.VMEM((8 * CH, 15 * CH), BF16),
                pltpu.VMEM((3, 3, 32, width + LANES), BF16),
                pltpu.VMEM((ACT + 2 * CH, TILE), BF16),
                pltpu.SemaphoreType.DMA((16,)),
                pltpu.SemaphoreType.DMA((16,)),
            ],
            compiler_params=pltpu.CompilerParams(collective_id=0, has_side_effects=True, vmem_limit_bytes=16 * 2**20),
        )(cube, aperture, meas, shears, steps, sw, sb, pw, pb, ow)
        return out.reshape(out.shape[0], 1, width)

    in_specs = (
        P("band", ("row", "col"), None),
        P(("row", "col"), None),
        P(("row", "col"), None),
        P("band"),
        P("band"),
        P(),
        P(),
        P(),
        P(),
        P(),
    )
    return jax.shard_map(
        on_device, mesh=mesh, in_specs=in_specs, out_specs=P("band", ("row", "col"), None), check_vma=False
    )
```
